32 devices in a mesh: parts: 2 (over x), sta: 16 (over z, y, core).
Axes of the slice: x: 2, y: 2, z: 4, core: 2. Of those that a mesh axis runs over, the one named last changes fastest.
Arguments:
- records: bfloat16 [32, 3, 2478], P('sta', None, 'parts'), parts along dimension 2, may hold values from -6 to 6
- templates: bfloat16 [32, 32, 3, 600], P(None, 'sta'), may hold values from -6 to 6
- shifts: int32 [32, 32], replicated, may hold values from 0 to 512, as said below
- present: int32 [32], replicated, may hold values 0 or 1
Outputs:
- detection: float32 [32, 256], P('sta', 'parts'), parts along dimension 1
The draws below stay inside these ranges and needn't reach their ends.
There are 2 independent parts, one for each index of `parts`. The reference program is written for one: setup_inputs(seed, part) draws one part's arguments, and reference() takes and returns one part's arrays. A program takes and returns all parts, laid end to end along the dimension named above; an argument that names none is the same for every part. Nothing has to cross between parts.
Inputs may be any that keep to these rules, and one draw needn't show every extreme that they name: `shifts`: for every template some station has moveout exactly 512 and some station moveout 0.
All inputs are finite; a program needn't handle non-finite values.
Results may differ from the reference program's by a relative error of at most 0.0029.
Values may be sent and summed in bfloat16 or wider, within the bound.
A program may use at most 64 MiB of HBM per device.

```python
import math
import jax
import jax.numpy as jnp
from jax import lax

LEN = 600
WIN = 640
MAXSHIFT = 512
STATIONS = 32
TEMPL = 32
SAMPLES = 1239


def draw_shifts(key, part):
    first = jax.random.fold_in(key, 11)
    second = jax.random.fold_in(key, 12)
    third = jax.random.fold_in(key, 13)
    base = jax.random.randint(first, (TEMPL, STATIONS), 0, MAXSHIFT + 1, dtype=jnp.int32)
    upper = jax.random.randint(second, (TEMPL,), 0, STATIONS, dtype=jnp.int32)
    lower = (upper + jax.random.randint(third, (TEMPL,), 1, STATIONS, dtype=jnp.int32)) % STATIONS
    column = jnp.arange(STATIONS, dtype=jnp.int32)[None, :]
    base = jnp.where(column == upper[:, None], MAXSHIFT, base)
    base = jnp.where(column == lower[:, None], 0, base)
    return base.astype(jnp.int32)


def plant(array, key, least, high):
    index_at = [jax.random.randint(jax.random.fold_in(key, axis), (), 0, length) for axis, length in enumerate(array.shape)]
    widest = array.shape.index(max(array.shape))
    beside = index_at[:widest] + [(index_at[widest] + 1) % array.shape[widest]] + index_at[widest + 1:]
    return array.at[tuple(index_at)].set(least).at[tuple(beside)].set(high)


def levels(key, shape, split, least, largest):
    def one(position, blocks):
        heights = jax.random.uniform(jax.random.fold_in(jax.random.fold_in(key, 6), position), (blocks,), jnp.float32, least / len(split), largest / len(split))
        return jnp.repeat(jnp.exp(heights), shape[position] // blocks).reshape((-1,) + (1,) * (len(shape) - position - 1))

    gain = one(*split[0])
    for cut in split[1:]:
        gain = gain * one(*cut)
    return gain


def gaussian(key, shape, spread, bound, shards=(), held_as=jnp.bfloat16):
    values = spread * jax.random.normal(key, shape, jnp.float32)
    if shards:
        values = values * levels(key, shape, shards, -0.22, 0.18)
    return jnp.clip(values, -bound, bound).astype(held_as)


def setup_inputs(seed: int = 0, part: int = 0) -> dict:
    keys = jax.random.split(jax.random.key(seed), 5)
    part_splits = jax.random.split(jax.random.fold_in(keys[4], part), 5)
    return {
        "records": gaussian(part_splits[0], (STATIONS, 3, SAMPLES), 1.0, 6.0, ((0, 16),)),
        "templates": gaussian(keys[1], (TEMPL, STATIONS, 3, LEN), 1.0, 6.0, ((1, 16),)),
        "shifts": draw_shifts(jax.random.fold_in(keys[4], 71), part),
        "present": plant((jax.random.randint(keys[3], (STATIONS,), 0, 4) < 3).astype(jnp.int32), jax.random.fold_in(keys[3], 1), 0, 1),
    }


def shift_rows(ncc, lags, count_out):

    def pick(row, lag):
        return lax.dynamic_slice_in_dim(row, lag.astype(jnp.int32), count_out, 0)
    return jax.vmap(pick)(ncc, lags)

def station_term(chosen, trace, lags, flag):
    values = chosen.astype(jnp.float32)
    power = lax.optimization_barrier(jnp.mean(values * values, axis=(1, 2), keepdims=True))
    normed = (values * lax.rsqrt(power + 1e-06)).astype(jnp.bfloat16)
    raw = lax.conv_general_dilated(trace[None], normed, (1,), 'VALID', dimension_numbers=('NCH', 'OIH', 'NCH'), preferred_element_type=jnp.float32)[0]
    energy = lax.optimization_barrier(jnp.sum(jnp.square(trace.astype(jnp.float32)), axis=0))
    running = jnp.concatenate([jnp.zeros((1,), jnp.float32), jnp.cumsum(energy)])
    window = (running[LEN:] - running[:-LEN]) / (3 * LEN)
    width = raw.shape[1]
    ncc = raw * lax.rsqrt(window + 1e-06)[None, :] / (3 * LEN)
    moved = shift_rows(ncc, lags, width - MAXSHIFT)
    return moved * flag.astype(jnp.float32)

def reference(records, templates, shifts, present):
    total = jnp.zeros((TEMPL, WIN - MAXSHIFT), jnp.float32)

    def visit(station, carry):
        chosen = lax.dynamic_index_in_dim(templates, station, 1, keepdims=False)
        trace = lax.dynamic_index_in_dim(records, station, 0, keepdims=False)
        lags = lax.dynamic_index_in_dim(shifts, station, 1, keepdims=False)
        flag = lax.dynamic_index_in_dim(present, station, 0, keepdims=False)
        return carry + station_term(chosen, trace, lags, flag)
    total = lax.fori_loop(0, STATIONS, visit, total)
    return total * math.sqrt(3 * LEN / STATIONS)
```

```python
import functools
import math

import jax
import jax.numpy as jnp
from jax import lax
from jax.experimental import pallas as pl
from jax.experimental.pallas import tpu as pltpu
from jax.sharding import PartitionSpec as P

LEN = 600
WIN = 640
MAXSHIFT = 512
OUT = WIN - MAXSHIFT
LANES = 128
SUB = 16
GROUPS = LANES // SUB
TAPS = -(-LEN // LANES)
LAGS = WIN + LANES
WIDE = WIN + TAPS * LANES
FULL, REST = divmod(LEN, LANES)
CHUNK = 8


def transposed(tiles, masks):
    tiles = list(tiles)
    size = GROUPS // 2
    while size:
        low = masks[size]
        for i in range(GROUPS):
            if not i & size:
                a, b = tiles[i], tiles[i + size]
                tiles[i] = jnp.where(low, a, pltpu.roll(b, SUB * size, 1))
                tiles[i + size] = jnp.where(low, pltpu.roll(a, LANES - SUB * size, 1), b)
        size //= 2
    return tiles


def kernel(
    n, rec_hbm, tem_hbm, shift_hbm, present_hbm, out_ref,
    rec_in, tem_in, shift_v, present_s, rec, turned, hank, energy, band, sums, inv_v, lag_v, pair, low_v, total, recv,
    in_sem, send_sem, recv_sem,
):
    me = lax.axis_index("sta")
    templ, local = tem_in.shape[1], tem_in.shape[2]
    rows = templ // n
    samples = rec_in.shape[2]
    stations = n * local
    R = CHUNK * local

    def load(src, dst, i):
        return pltpu.make_async_copy(src, dst, in_sem.at[i])

    def tem_load(c, start, count, i):
        return load(tem_hbm.at[pl.ds(start, count), c], tem_in.at[c, pl.ds(start, count)], i)

    rec_load = load(rec_hbm, rec_in, 0)
    shift_load = load(shift_hbm, shift_v, 1)
    present_load = load(present_hbm, present_s, 2)
    first = [tem_load(c, 0, CHUNK, 3 + c) for c in range(3)]
    others = [tem_load(c, CHUNK, templ - CHUNK, 6 + c) for c in range(3)] if templ > CHUNK else []
    for x in [rec_load, *first, shift_load, present_load, *others]:
        x.start()

    barrier = pltpu.get_barrier_semaphore()
    for step in range(1, n):
        pl.semaphore_signal(
            barrier, inc=1, device_id={"sta": lax.rem(me + step, n)},
            device_id_type=pl.DeviceIdType.MESH,
        )

    at = lax.broadcasted_iota(jnp.int32, (LANES, LANES), 0)
    to = lax.broadcasted_iota(jnp.int32, (LANES, LANES), 1)
    for i, mask in enumerate([at >= to, at >= 0, at < to + REST, at < to + (REST - LANES)]):
        band[:, i * LANES : (i + 1) * LANES] = mask.astype(jnp.float32).astype(jnp.bfloat16)
    energy[...] = jnp.zeros_like(energy)
    rec[...] = jnp.zeros_like(rec)
    lane = lax.broadcasted_iota(jnp.int32, (R, LANES), 1)
    which = lax.broadcasted_iota(jnp.int32, (R, LANES), 0) % local
    block = lane // SUB

    def by_station(values):
        out = values[0]
        for s in range(1, local):
            out = jnp.where(which == s, values[s], out)
        return out

    sizes = [1 << i for i in range(GROUPS.bit_length() - 1)]
    for i, size in enumerate(sizes):
        low_v[i] = jnp.where(block % (2 * size) < size, 1.0, 0.0).astype(jnp.bfloat16)
    masks = {size: low_v[i] > 0 for i, size in enumerate(sizes)}

    rec_load.wait()
    waves = [rec_in[c].astype(jnp.float32) for c in range(3)]
    for c in range(3):
        rec[c * local : (c + 1) * local, 0:samples] = waves[c]
    power = waves[0] * waves[0] + waves[1] * waves[1] + waves[2] * waves[2]
    for q in range(-(-samples // LANES)):
        span = min(LANES, samples - q * LANES)
        energy[q * local : (q + 1) * local, 0:span] = power[:, q * LANES : q * LANES + span]
    flip = LANES - 1 - lax.broadcasted_iota(jnp.int32, (rec.shape[0], LANES), 1)
    for i in range(0, WIDE, LANES):
        turned[:, WIDE - LANES - i : WIDE - i] = jnp.take_along_axis(rec[:, i : i + LANES], flip, axis=1)
    for s in range(local):
        for c in range(3):
            row = jnp.broadcast_to(turned[c * local + s : c * local + s + 1, :], (SUB, WIDE))
            hank[s, c] = pltpu.roll(row, 0, 1, stride=1, stride_axis=0).astype(jnp.bfloat16)

    whole = energy[...]
    count = whole.shape[0]
    high = whole.astype(jnp.bfloat16)
    left = whole - high.astype(jnp.float32)
    middle = left.astype(jnp.bfloat16)
    low = (left - middle.astype(jnp.float32)).astype(jnp.bfloat16)
    split = jnp.dot(
        jnp.concatenate([high, middle, low], axis=0), band[...], preferred_element_type=jnp.float32
    )
    sums[...] = split[:count] + split[count : 2 * count] + split[2 * count :]
    lag_rows = local * (WIN // LANES)

    def part(kind, behind):
        return sums[behind * local : behind * local + lag_rows, kind * LANES : (kind + 1) * LANES]

    window = part(0, 0) + part(2, FULL) + part(3, FULL + 1)
    for i in range(1, FULL):
        window = window + part(1, i)
    inv_v[0:lag_rows, :] = lax.rsqrt(window / (3 * LEN) + 1e-06)
    inv_tiles = [
        by_station([jnp.broadcast_to(inv_v[i * local + s : i * local + s + 1, :], (R, LANES)) for s in range(local)])
        for i in range(WIN // LANES)
    ]

    shift_load.wait()
    present_load.wait()
    lags_all = shift_v[...].astype(jnp.float32)
    column = lax.broadcasted_iota(jnp.int32, lags_all.shape, 1)
    scale = math.sqrt(3 * LEN / stations) / (3 * LEN)
    flags = []
    for s in range(local):
        lag = jnp.sum(jnp.where(column == me * local + s, lags_all, 0.0), axis=1, keepdims=True)
        lag_v[pl.ds(s, templ, stride=local), :] = jnp.broadcast_to(lag.astype(jnp.int32), (templ, LANES))
        flags.append(jnp.full((R, LANES), present_s[me * local + s].astype(jnp.float32) * scale))
    flag = by_station(flags)

    def picked(tiles, pos, back):
        coarse, fine = pos // LANES, pos % LANES
        near, far = tiles[0], tiles[1]
        for i in range(1, len(tiles) - 1):
            near = jnp.where(coarse == i, tiles[i], near)
            far = jnp.where(coarse == i, tiles[i + 1], far)
        place, source = lane, (lane + fine) % LANES
        if back:
            place, source = LANES - 1 - place, LANES - 1 - source
        return jnp.take_along_axis(jnp.where(place >= fine, near, far), source, axis=1)

    def work(k):
        t0 = k * CHUNK
        tiles = []
        square = jnp.zeros((R, LANES), jnp.float32)
        for c in range(3):
            view = tem_in.at[c].reshape(templ * local, LEN)
            for a in range(TAPS):
                span = min(LANES, LEN - a * LANES)
                x = view[t0 * local : t0 * local + R, a * LANES : a * LANES + span]
                if span < LANES:
                    x = jnp.concatenate([x, jnp.zeros((R, LANES - span), x.dtype)], axis=1)
                tiles.append(x)
                y = x.astype(jnp.float32)
                square = square + y * y
        gain = lax.rsqrt(jnp.sum(square, axis=1, keepdims=True) / (3 * LEN) + 1e-06)
        blank = jnp.zeros((R, LANES), jnp.bfloat16)
        halves = []
        for g in range(0, len(tiles), GROUPS):
            some = tiles[g : g + GROUPS]
            halves.append(transposed(some + [blank] * (GROUPS - len(some)), masks))
        depth = 3 * TAPS * SUB
        left = jnp.concatenate(
            [jnp.concatenate([h[j] for h in halves], axis=1) for j in range(GROUPS)], axis=0
        )[:, :depth]
        both = []
        for s in range(local):
            right = jnp.concatenate(
                [hank[s, c, :, WIDE - LAGS - a * LANES : WIDE - a * LANES] for c in range(3) for a in range(TAPS)], axis=0
            )
            both.append(jnp.dot(left, right, preferred_element_type=jnp.float32))
        lag = lag_v[t0 * local : t0 * local + R, :]
        acc = jnp.zeros((R, LANES), jnp.float32)
        for j in range(GROUPS):
            mixed = by_station_tiles([b[j * R : (j + 1) * R] for b in both])
            acc = acc + picked(mixed[::-1], lag + j * SUB, True)
        norm = picked(inv_tiles + [inv_tiles[-1]], lag, False)
        pair[...] = acc * norm * (gain * flag)
        done = pair[pl.ds(0, CHUNK, stride=local), :]
        for s in range(1, local):
            done = done + pair[pl.ds(s, CHUNK, stride=local), :]
        for i in range(CHUNK // rows):
            total[t0 // rows + i] = done[i * rows : (i + 1) * rows]

    def by_station_tiles(parts):
        return [
            by_station([p[:, i * LANES : (i + 1) * LANES] for p in parts]) for i in range(LAGS // LANES)
        ]

    def send(k):
        for i in range(CHUNK // rows):
            d = k * (CHUNK // rows) + i

            @pl.when(me != d)
            def _():
                pltpu.make_async_remote_copy(
                    src_ref=total.at[d], dst_ref=recv.at[lax.rem(d - me + n, n)],
                    send_sem=send_sem, recv_sem=recv_sem,
                    device_id={"sta": d}, device_id_type=pl.DeviceIdType.MESH,
                ).start()

    for x in first:
        x.wait()
    work(0)
    pl.semaphore_wait(barrier, n - 1)
    send(0)
    for x in others:
        x.wait()
    for k in range(1, templ // CHUNK):
        work(k)
        send(k)
    rest = recv.at[pl.ds(1, n - 1)]
    pltpu.make_async_copy(rest, rest, recv_sem).wait()
    pltpu.make_async_copy(rest, rest, send_sem).wait()
    out_ref[...] = total[me] + jnp.sum(recv[pl.ds(1, n - 1)], axis=0)


def body(records, templates, shifts, present):
    n = lax.axis_size("sta")
    templ, local = templates.shape[0], templates.shape[1]
    rows = templ // n
    records = records.transpose(1, 0, 2)
    templates = templates.transpose(0, 2, 1, 3)
    energy_rows = -(-local * (WIDE // LANES) // 16) * 16
    hbm = pl.BlockSpec(memory_space=pl.ANY)
    return pl.pallas_call(
        functools.partial(kernel, n),
        out_shape=jax.ShapeDtypeStruct((rows, OUT), jnp.float32),
        in_specs=[hbm] * 4,
        out_specs=pl.BlockSpec(memory_space=pltpu.VMEM),
        scratch_shapes=[
            pltpu.VMEM(records.shape, records.dtype),
            pltpu.VMEM((3, templ, local, LEN), templates.dtype),
            pltpu.VMEM(shifts.shape, shifts.dtype),
            pltpu.SMEM(present.shape, present.dtype),
            pltpu.VMEM((-(-3 * local // 8) * 8, WIDE), jnp.float32),
            pltpu.VMEM((-(-3 * local // 8) * 8, WIDE), jnp.float32),
            pltpu.VMEM((local, 3, SUB, WIDE), jnp.bfloat16),
            pltpu.VMEM((energy_rows, LANES), jnp.float32),
            pltpu.VMEM((LANES, 4 * LANES), jnp.bfloat16),
            pltpu.VMEM((energy_rows, 4 * LANES), jnp.float32),
            pltpu.VMEM((energy_rows, LANES), jnp.float32),
            pltpu.VMEM((templ * local, LANES), jnp.int32),
            pltpu.VMEM((CHUNK * local, LANES), jnp.float32),
            pltpu.VMEM((GROUPS.bit_length() - 1, CHUNK * local, LANES), jnp.bfloat16),
            pltpu.VMEM((n, rows, OUT), jnp.float32),
            pltpu.VMEM((n, rows, OUT), jnp.float32),
            pltpu.SemaphoreType.DMA((9,)),
            pltpu.SemaphoreType.DMA,
            pltpu.SemaphoreType.DMA,
        ],
        compiler_params=pltpu.CompilerParams(collective_id=0, vmem_limit_bytes=16 << 20, has_side_effects=True),
    )(*[
        pltpu.with_memory_space_constraint(x, pltpu.HBM) for x in (records, templates, shifts, present)])


def solution(mesh):
    placed = (P("sta", None, "parts"), P(None, "sta", None, None), P(), P())
    return jax.shard_map(
        body, mesh=mesh, in_specs=placed, out_specs=P("sta", "parts"), check_vma=False
    )
```

```python
import functools
import math

import jax
import jax.numpy as jnp
from jax import lax
from jax.experimental import pallas as pl
from jax.experimental.pallas import tpu as pltpu
from jax.sharding import PartitionSpec as P

LEN = 600
WIN = 640
MAXSHIFT = 512
OUT = WIN - MAXSHIFT
LANES = 128
SUB = 16
GROUPS = LANES // SUB
TAPS = -(-LEN // LANES)
LAGS = WIN + LANES
WIDE = WIN + TAPS * LANES
FULL, REST = divmod(LEN, LANES)
CHUNK = 8
LEVELS = (7,)


def transposed(tiles, part_v):
    for level, bits in enumerate(LEVELS):
        parts = part_v[level]
        moves = [m for m in range(GROUPS) if m & bits == m]
        out = []
        for i in range(GROUPS):
            mixed = None
            for m in moves:
                x = tiles[i & ~bits | m]
                turn = SUB * (m - (i & bits)) % LANES
                x = pltpu.roll(x, turn, 1) if turn else x
                mixed = x if mixed is None else jnp.where(parts == m, x, mixed)
            out.append(mixed)
        tiles = out
    return tiles


def kernel(
    n, rec_hbm, tem_hbm, shift_hbm, present_hbm, out_ref,
    rec_in, tem_in, tem, shift_v, present_s, rec, hank, energy, band, sums, inv_v, lag_v, part_v, total, recv,
    in_sem, send_sem, recv_sem, ready_sem,
):
    me = lax.axis_index("sta")
    templ, local = tem_in.shape[0], tem_in.shape[2]
    rows = templ // n
    samples = rec_in.shape[2]
    stations = n * local

    def load(src, dst, i):
        return pltpu.make_async_copy(src, dst, in_sem.at[i])

    def tem_load(start, count, i):
        return load(tem_hbm.at[pl.ds(start, count)], tem_in.at[pl.ds(start, count)], i)

    rec_load = load(rec_hbm, rec_in, 0)
    shift_load = load(shift_hbm, shift_v, 1)
    present_load = load(present_hbm, present_s, 2)
    first = [tem_load(0, CHUNK, 3)]
    others = [tem_load(CHUNK, templ - CHUNK, 4)] if templ > CHUNK else []
    for x in [rec_load, *first, shift_load, present_load, *others]:
        x.start()

    barrier = pltpu.get_barrier_semaphore()

    def greet(d, carry):
        pl.semaphore_signal(barrier, inc=1, device_id={"sta": d}, device_id_type=pl.DeviceIdType.MESH)
        return carry

    def answer(d, carry):
        pl.semaphore_signal(
            ready_sem, inc=1, device_id={"sta": d}, device_id_type=pl.DeviceIdType.MESH
        )
        return carry

    lax.fori_loop(me + 1, n, greet, 0)

    @pl.when(me > 0)
    def _():
        pl.semaphore_wait(barrier, me)

    lax.fori_loop(0, me, answer, 0)

    at = lax.broadcasted_iota(jnp.int32, (LANES, LANES), 0)
    to = lax.broadcasted_iota(jnp.int32, (LANES, LANES), 1)
    for i, mask in enumerate([at >= to, at >= 0, at < to + REST, at < to + (REST - LANES)]):
        band[:, i * LANES : (i + 1) * LANES] = mask.astype(jnp.float32).astype(jnp.bfloat16)
    energy[...] = jnp.zeros_like(energy)
    rec[...] = jnp.zeros_like(rec)
    for c in range(3):
        tem[c * TAPS + FULL] = jnp.zeros((templ * local, LANES), tem.dtype)
    lane = lax.broadcasted_iota(jnp.int32, (CHUNK, LANES), 1)
    block = lax.broadcasted_iota(jnp.int32, (2 * CHUNK, LANES), 1) // SUB

    for level, bits in enumerate(LEVELS):
        part_v[level] = (block & bits).astype(jnp.float32).astype(jnp.bfloat16)

    for x in [rec_load, shift_load, present_load, *first]:
        x.wait()
    waves = [rec_in[c].astype(jnp.float32) for c in range(3)]
    for c in range(3):
        rec[c * local : (c + 1) * local, 0:samples] = waves[c]
    power = waves[0] * waves[0] + waves[1] * waves[1] + waves[2] * waves[2]
    for q in range(-(-samples // LANES)):
        span = min(LANES, samples - q * LANES)
        energy[q * local : (q + 1) * local, 0:span] = power[:, q * LANES : q * LANES + span]
    flip = 7 - lax.broadcasted_iota(jnp.int32, (8, LANES), 0)
    for s in range(local):
        for c in range(3):
            row = jnp.broadcast_to(rec[c * local + s : c * local + s + 1, :], (SUB, WIDE))
            slid = pltpu.roll(row, WIDE - SUB + 1, 1, stride=1, stride_axis=0)
            for i in range(0, WIDE, LANES):
                hank[s, c, :, i : i + LANES] = jnp.concatenate(
                    [jnp.take_along_axis(slid[r : r + 8, i : i + LANES], flip, axis=0) for r in (8, 0)], axis=0
                ).astype(jnp.bfloat16)

    whole = energy[...]
    count = whole.shape[0]
    high = whole.astype(jnp.bfloat16)
    left = whole - high.astype(jnp.float32)
    middle = left.astype(jnp.bfloat16)
    low = (left - middle.astype(jnp.float32)).astype(jnp.bfloat16)
    split = jnp.dot(
        jnp.concatenate([high, middle, low], axis=0), band[...], preferred_element_type=jnp.float32
    )
    sums[...] = split[:count] + split[count : 2 * count] + split[2 * count :]
    lag_rows = local * (WIN // LANES)

    def part(kind, behind):
        return sums[behind * local : behind * local + lag_rows, kind * LANES : (kind + 1) * LANES]

    window = part(0, 0) + part(2, FULL) + part(3, FULL + 1)
    for i in range(1, FULL):
        window = window + part(1, i)
    inv_v[0:lag_rows, :] = lax.rsqrt(window / (3 * LEN) + 1e-06)

    def inverse(s):
        return [
            jnp.broadcast_to(inv_v[i * local + s : i * local + s + 1, :], (CHUNK, LANES))
            for i in range(WIN // LANES)
        ]


    lags_all = shift_v[...].astype(jnp.float32)
    column = lax.broadcasted_iota(jnp.int32, lags_all.shape, 1)
    scale = math.sqrt(3 * LEN / stations) / (3 * LEN)
    flags = []
    for s in range(local):
        lag = jnp.sum(jnp.where(column == me * local + s, lags_all, 0.0), axis=1, keepdims=True)
        lag_v[s] = jnp.broadcast_to(lag.astype(jnp.int32), (templ, LANES))
        flags.append(present_s[me * local + s].astype(jnp.float32) * scale)

    def picked(tiles, pos, back):
        coarse, fine = pos >> (LANES.bit_length() - 1), pos & (LANES - 1)
        near, far = tiles[0], tiles[1]
        for i in range(1, len(tiles) - 1):
            near = jnp.where(coarse == i, tiles[i], near)
            far = jnp.where(coarse == i, tiles[i + 1], far)
        place, source = lane, (lane + fine) & (LANES - 1)
        if back:
            place, source = LANES - 1 - place, LANES - 1 - source
        return jnp.take_along_axis(jnp.where(place >= fine, near, far), source, axis=1)

    def work(k):
        t0 = k * CHUNK
        for t in range(t0, t0 + CHUNK):
            for c in range(3):
                wave = tem_in[t, c].astype(jnp.float32)
                for a in range(TAPS):
                    span = min(LANES, LEN - a * LANES)
                    tem[c * TAPS + a, t * local : (t + 1) * local, 0:span] = wave[:, a * LANES : a * LANES + span]
        done = jnp.zeros((CHUNK, LANES), jnp.float32)
        for s in range(local):
            tiles = [tem[i, pl.ds(t0 * local + s, CHUNK, stride=local), :] for i in range(3 * TAPS)]
            square = sum(x * x for x in tiles)
            gain = lax.rsqrt(jnp.sum(square, axis=1, keepdims=True) / (3 * LEN) + 1e-06) * flags[s]
            tiles = tiles + [jnp.zeros((CHUNK, LANES), jnp.float32)] * (2 * GROUPS - len(tiles))
            pairs = [
                jnp.concatenate([tiles[i], tiles[i + GROUPS]], axis=0).astype(jnp.bfloat16)
                for i in range(GROUPS)
            ]
            pairs = [x.astype(jnp.float32) for x in transposed(pairs, part_v)]
            left = jnp.concatenate(
                [jnp.concatenate([x[:CHUNK], x[CHUNK:]], axis=1) for x in pairs], axis=0
            )[:, : 3 * TAPS * SUB].astype(jnp.bfloat16)
            right = jnp.concatenate(
                [hank[s, c, :, a * LANES : a * LANES + LAGS] for c in range(3) for a in range(TAPS)],
                axis=0,
            )
            both = jnp.dot(left, right, preferred_element_type=jnp.float32)
            lag = lag_v[s, t0 : t0 + CHUNK, :]
            acc = jnp.zeros((CHUNK, LANES), jnp.float32)
            for j in range(GROUPS):
                part = both[j * CHUNK : (j + 1) * CHUNK]
                parts = [part[:, i * LANES : (i + 1) * LANES] for i in range(LAGS // LANES)]
                acc = acc + picked(parts, lag + j * SUB, False)
            window = inverse(s)
            norm = picked(window + [window[-1]], lag, False)
            done = done + acc * norm * gain
        for i in range(CHUNK // rows):
            total[t0 // rows + i] = done[i * rows : (i + 1) * rows]

    def send(d):
        pltpu.make_async_remote_copy(
            src_ref=total.at[d], dst_ref=recv.at[lax.rem(d - me + n, n)],
            send_sem=send_sem, recv_sem=recv_sem,
            device_id={"sta": d}, device_id_type=pl.DeviceIdType.MESH,
        ).start()

    def send_back(k):
        for d in range(k * CHUNK // rows, (k + 1) * CHUNK // rows):

            @pl.when(d < me)
            def _():
                send(d)

    def send_on(d, carry):
        send(d)
        return carry

    work(0)
    send_back(0)
    for x in others:
        x.wait()
    for k in range(1, templ // CHUNK):
        work(k)
        send_back(k)

    @pl.when(me < n - 1)
    def _():
        pl.semaphore_wait(ready_sem, n - 1 - me)

    lax.fori_loop(me + 1, n, send_on, 0)
    rest = recv.at[pl.ds(1, n - 1)]
    pltpu.make_async_copy(rest, rest, recv_sem).wait()
    pltpu.make_async_copy(rest, rest, send_sem).wait()
    out_ref[...] = total[me] + jnp.sum(recv[pl.ds(1, n - 1)], axis=0)


def body(records, templates, shifts, present):
    n = lax.axis_size("sta")
    templ, local = templates.shape[0], templates.shape[1]
    rows = templ // n
    records = records.transpose(1, 0, 2)
    templates = templates.transpose(0, 2, 1, 3)
    energy_rows = -(-local * (WIDE // LANES) // 16) * 16
    hbm = pl.BlockSpec(memory_space=pl.ANY)
    return pl.pallas_call(
        functools.partial(kernel, n),
        out_shape=jax.ShapeDtypeStruct((rows, OUT), jnp.float32),
        in_specs=[hbm] * 4,
        out_specs=pl.BlockSpec(memory_space=pltpu.VMEM),
        scratch_shapes=[
            pltpu.VMEM(records.shape, records.dtype),
            pltpu.VMEM(templates.shape, templates.dtype),
            pltpu.VMEM((3 * TAPS, templ * local, LANES), jnp.float32),
            pltpu.VMEM(shifts.shape, shifts.dtype),
            pltpu.SMEM(present.shape, present.dtype),
            pltpu.VMEM((-(-3 * local // 8) * 8, WIDE), jnp.float32),
            pltpu.VMEM((local, 3, SUB, WIDE), jnp.bfloat16),
            pltpu.VMEM((energy_rows, LANES), jnp.float32),
            pltpu.VMEM((LANES, 4 * LANES), jnp.bfloat16),
            pltpu.VMEM((energy_rows, 4 * LANES), jnp.float32),
            pltpu.VMEM((energy_rows, LANES), jnp.float32),
            pltpu.VMEM((local, templ, LANES), jnp.int32),
            pltpu.VMEM((len(LEVELS), 2 * CHUNK, LANES), jnp.bfloat16),
            pltpu.VMEM((n, rows, OUT), jnp.float32),
            pltpu.VMEM((n, rows, OUT), jnp.float32),
            pltpu.SemaphoreType.DMA((5,)),
            pltpu.SemaphoreType.DMA,
            pltpu.SemaphoreType.DMA,
            pltpu.SemaphoreType.REGULAR,
        ],
        compiler_params=pltpu.CompilerParams(collective_id=0, vmem_limit_bytes=16 << 20, has_side_effects=True),
    )(*[
        pltpu.with_memory_space_constraint(x, pltpu.HBM) for x in (records, templates, shifts, present)])


def solution(mesh):
    placed = (P("sta", None, "parts"), P(None, "sta", None, None), P(), P())
    return jax.shard_map(
        body, mesh=mesh, in_specs=placed, out_specs=P("sta", "parts"), check_vma=False
    )
```

```python
import functools
import math

import jax
import jax.numpy as jnp
from jax import lax
from jax.experimental import pallas as pl
from jax.experimental.pallas import tpu as pltpu
from jax.sharding import PartitionSpec as P

LEN = 600
WIN = 640
MAXSHIFT = 512
OUT = WIN - MAXSHIFT
LANES = 128
SUB = 16
GROUPS = LANES // SUB
TAPS = -(-LEN // LANES)
LAGS = WIN + LANES
WIDE = WIN + TAPS * LANES
FULL, REST = divmod(LEN, LANES)
CHUNK = 8
LEVELS = (7,)


def transposed(tiles, part_v):
    for level, bits in enumerate(LEVELS):
        parts = part_v[level]
        moves = [m for m in range(GROUPS) if m & bits == m]
        out = []
        for i in range(GROUPS):
            mixed = None
            for m in moves:
                x = tiles[i & ~bits | m]
                turn = SUB * (m - (i & bits)) % LANES
                x = pltpu.roll(x, turn, 1) if turn else x
                mixed = x if mixed is None else jnp.where(parts == m, x, mixed)
            out.append(mixed)
        tiles = out
    return tiles


def kernel(
    n, rec_hbm, tem_hbm, shift_hbm, present_hbm, out_ref,
    rec_in, tem_in, tem, shift_v, present_s, rec, hank, energy, band, sums, inv_v, lag_v, pair, part_v, total, recv,
    in_sem, send_sem, recv_sem, ready_sem,
):
    me = lax.axis_index("sta")
    templ, local = tem_in.shape[0], tem_in.shape[2]
    rows = templ // n
    samples = rec_in.shape[2]
    stations = n * local

    def load(src, dst, i):
        return pltpu.make_async_copy(src, dst, in_sem.at[i])

    def tem_load(start, count, i):
        return load(tem_hbm.at[pl.ds(start, count)], tem_in.at[pl.ds(start, count)], i)

    rec_load = pltpu.make_async_copy(rec_hbm, rec_in, send_sem)
    shift_load = load(shift_hbm, shift_v, 0)
    present_load = load(present_hbm, present_s, 1)
    small = 8 // local
    first = tem_load(0, small, 2)
    others = tem_load(small, templ - small, 3)
    for x in [first, rec_load, shift_load, present_load, others]:
        x.start()

    barrier = pltpu.get_barrier_semaphore()

    def greet(d, carry):
        pl.semaphore_signal(barrier, inc=1, device_id={"sta": d}, device_id_type=pl.DeviceIdType.MESH)
        return carry

    def answer(d, carry):
        pl.semaphore_signal(
            ready_sem, inc=1, device_id={"sta": d}, device_id_type=pl.DeviceIdType.MESH
        )
        return carry

    lax.fori_loop(me + 1, n, greet, 0)

    @pl.when(me > 0)
    def _():
        pl.semaphore_wait(barrier, me)

    lax.fori_loop(0, me, answer, 0)

    at = lax.broadcasted_iota(jnp.int32, (LANES, LANES), 0)
    to = lax.broadcasted_iota(jnp.int32, (LANES, LANES), 1)
    for i, mask in enumerate([at >= to, at >= 0, at < to + REST, at < to + (REST - LANES)]):
        band[:, i * LANES : (i + 1) * LANES] = mask.astype(jnp.float32).astype(jnp.bfloat16)
    energy[...] = jnp.zeros_like(energy)
    rec[...] = jnp.zeros_like(rec)
    for c in range(3):
        tem[c * TAPS + FULL] = jnp.zeros((templ * local, LANES), tem.dtype)
    lane = lax.broadcasted_iota(jnp.int32, (CHUNK, LANES), 1)
    block = lax.broadcasted_iota(jnp.int32, (2 * CHUNK, LANES), 1) // SUB

    for level, bits in enumerate(LEVELS):
        part_v[level] = (block & bits).astype(jnp.float32).astype(jnp.bfloat16)

    for x in [rec_load, shift_load, present_load, first]:
        x.wait()
    waves = [rec_in[c].astype(jnp.float32) for c in range(3)]
    for c in range(3):
        rec[c * local : (c + 1) * local, 0:samples] = waves[c]
    power = waves[0] * waves[0] + waves[1] * waves[1] + waves[2] * waves[2]
    for q in range(-(-samples // LANES)):
        span = min(LANES, samples - q * LANES)
        energy[q * local : (q + 1) * local, 0:span] = power[:, q * LANES : q * LANES + span]
    flip = 7 - lax.broadcasted_iota(jnp.int32, (8, LANES), 0)
    for s in range(local):
        for c in range(3):
            row = jnp.broadcast_to(rec[c * local + s : c * local + s + 1, :], (SUB, WIDE))
            slid = pltpu.roll(row, WIDE - SUB + 1, 1, stride=1, stride_axis=0)
            for i in range(0, WIDE, LANES):
                hank[s, c, :, i : i + LANES] = jnp.concatenate(
                    [jnp.take_along_axis(slid[r : r + 8, i : i + LANES], flip, axis=0) for r in (8, 0)], axis=0
                ).astype(jnp.bfloat16)

    whole = energy[...]
    count = whole.shape[0]
    high = whole.astype(jnp.bfloat16)
    left = whole - high.astype(jnp.float32)
    middle = left.astype(jnp.bfloat16)
    low = (left - middle.astype(jnp.float32)).astype(jnp.bfloat16)
    split = jnp.dot(
        jnp.concatenate([high, middle, low], axis=0), band[...], preferred_element_type=jnp.float32
    )
    sums[...] = split[:count] + split[count : 2 * count] + split[2 * count :]
    lag_rows = local * (WIN // LANES)

    def part(kind, behind):
        return sums[behind * local : behind * local + lag_rows, kind * LANES : (kind + 1) * LANES]

    window = part(0, 0) + part(2, FULL) + part(3, FULL + 1)
    for i in range(1, FULL):
        window = window + part(1, i)
    inv_v[0:lag_rows, :] = lax.rsqrt(window / (3 * LEN) + 1e-06)

    def inverse(s):
        return [
            jnp.broadcast_to(inv_v[i * local + s : i * local + s + 1, :], (CHUNK, LANES))
            for i in range(WIN // LANES)
        ]


    lags_all = shift_v[...].astype(jnp.float32)
    column = lax.broadcasted_iota(jnp.int32, lags_all.shape, 1)
    scale = math.sqrt(3 * LEN / stations) / (3 * LEN)
    flags = []
    for s in range(local):
        lag = jnp.sum(jnp.where(column == me * local + s, lags_all, 0.0), axis=1, keepdims=True)
        lag_v[pl.ds(s, templ, stride=local), :] = jnp.broadcast_to(lag.astype(jnp.int32), (templ, LANES))
        flags.append(present_s[me * local + s].astype(jnp.float32) * scale)

    which = lax.broadcasted_iota(jnp.int32, (8, LANES), 0) % local

    def by_station(values):
        out = values[0]
        for s in range(1, local):
            out = jnp.where(which == s, values[s], out)
        return out

    def picked(tiles, pos):
        coarse, fine = pos >> (LANES.bit_length() - 1), pos & (LANES - 1)
        near, far = tiles[0], tiles[1]
        for i in range(1, len(tiles) - 1):
            near = jnp.where(coarse == i, tiles[i], near)
            far = jnp.where(coarse == i, tiles[i + 1], far)
        return jnp.take_along_axis(
            jnp.where(lane >= fine, near, far), (lane + fine) & (LANES - 1), axis=1
        )

    def stage(t0, count):
        for t in range(t0, t0 + count):
            for c in range(3):
                wave = tem_in[t, c].astype(jnp.float32)
                for a in range(TAPS):
                    span = min(LANES, LEN - a * LANES)
                    tem[c * TAPS + a, t * local : (t + 1) * local, 0:span] = wave[:, a * LANES : a * LANES + span]

    def operands(tiles):
        square = sum(x * x for x in tiles)
        gain = lax.rsqrt(jnp.sum(square, axis=1, keepdims=True) / (3 * LEN) + 1e-06)
        tiles = tiles + [jnp.zeros((8, LANES), jnp.float32)] * (2 * GROUPS - len(tiles))
        pairs = [
            jnp.concatenate([tiles[i], tiles[i + GROUPS]], axis=0).astype(jnp.bfloat16)
            for i in range(GROUPS)
        ]
        pairs = [x.astype(jnp.float32) for x in transposed(pairs, part_v)]
        left = jnp.concatenate([jnp.concatenate([x[:8], x[8:]], axis=1) for x in pairs], axis=0)
        return gain, left[:, : 3 * TAPS * SUB].astype(jnp.bfloat16)

    def raw(left, s):
        right = jnp.concatenate(
            [hank[s, c, :, a * LANES : a * LANES + LAGS] for c in range(3) for a in range(TAPS)], axis=0
        )
        both = jnp.dot(left, right, preferred_element_type=jnp.float32)
        return [
            [both[j * 8 : j * 8 + 8, i * LANES : (i + 1) * LANES] for i in range(LAGS // LANES)]
            for j in range(GROUPS)
        ]

    def keep(done, t0):
        for i in range(done.shape[0] // rows):
            total[t0 // rows + i] = done[i * rows : (i + 1) * rows]

    def stacked(parts, lag, window):
        acc = sum(picked(parts[j], lag + j * SUB) for j in range(GROUPS))
        return acc * picked(window + [window[-1]], lag)

    def work_small(t0):
        count = 8 // local
        stage(t0, count)
        first = t0 * local
        gain, left = operands([tem[i, first : first + 8, :] for i in range(3 * TAPS)])
        raws = [raw(left, s) for s in range(local)]
        parts = [
            [by_station([r[j][i] for r in raws]) for i in range(LAGS // LANES)] for j in range(GROUPS)
        ]
        window = [by_station(list(x)) for x in zip(*[inverse(s) for s in range(local)])]
        flag = by_station([jnp.full((8, LANES), f) for f in flags])
        pair[...] = stacked(parts, lag_v[first : first + 8, :], window) * (gain * flag)
        keep(sum(pair[pl.ds(s, count, stride=local), :] for s in range(local)), t0)

    def work(t0):
        stage(t0, CHUNK)
        done = jnp.zeros((CHUNK, LANES), jnp.float32)
        for s in range(local):
            mine = pl.ds(t0 * local + s, CHUNK, stride=local)
            gain, left = operands([tem[i, mine, :] for i in range(3 * TAPS)])
            done = done + stacked(raw(left, s), lag_v[mine, :], inverse(s)) * (gain * flags[s])
        keep(done, t0)

    def send(d):
        pltpu.make_async_remote_copy(
            src_ref=total.at[d], dst_ref=recv.at[lax.rem(d - me + n, n)],
            send_sem=send_sem, recv_sem=recv_sem,
            device_id={"sta": d}, device_id_type=pl.DeviceIdType.MESH,
        ).start()

    def send_back(t0, count):
        for d in range(t0 // rows, (t0 + count) // rows):

            @pl.when(d < me)
            def _():
                send(d)

    def send_on(d, carry):
        send(d)
        return carry

    work_small(0)
    send_back(0, small)
    others.wait()
    for t0 in range(small, CHUNK, small):
        work_small(t0)
        send_back(t0, small)
    for t0 in range(CHUNK, templ, CHUNK):
        work(t0)
        send_back(t0, CHUNK)

    @pl.when(me < n - 1)
    def _():
        pl.semaphore_wait(ready_sem, n - 1 - me)

    lax.fori_loop(me + 1, n, send_on, 0)
    rest = recv.at[pl.ds(1, n - 1)]
    pltpu.make_async_copy(rest, rest, recv_sem).wait()
    pltpu.make_async_copy(rest, rest, send_sem).wait()
    out_ref[...] = total[me] + jnp.sum(recv[pl.ds(1, n - 1)], axis=0)


def body(records, templates, shifts, present):
    n = lax.axis_size("sta")
    templ, local = templates.shape[0], templates.shape[1]
    rows = templ // n
    records = records.transpose(1, 0, 2)
    templates = templates.transpose(0, 2, 1, 3)
    energy_rows = -(-local * (WIDE // LANES) // 16) * 16
    hbm = pl.BlockSpec(memory_space=pl.ANY)
    return pl.pallas_call(
        functools.partial(kernel, n),
        out_shape=jax.ShapeDtypeStruct((rows, OUT), jnp.float32),
        in_specs=[hbm] * 4,
        out_specs=pl.BlockSpec(memory_space=pltpu.VMEM),
        scratch_shapes=[
            pltpu.VMEM(records.shape, records.dtype),
            pltpu.VMEM(templates.shape, templates.dtype),
            pltpu.VMEM((3 * TAPS, templ * local, LANES), jnp.float32),
            pltpu.VMEM(shifts.shape, shifts.dtype),
            pltpu.SMEM(present.shape, present.dtype),
            pltpu.VMEM((-(-3 * local // 8) * 8, WIDE), jnp.float32),
            pltpu.VMEM((local, 3, SUB, WIDE), jnp.bfloat16),
            pltpu.VMEM((energy_rows, LANES), jnp.float32),
            pltpu.VMEM((LANES, 4 * LANES), jnp.bfloat16),
            pltpu.VMEM((energy_rows, 4 * LANES), jnp.float32),
            pltpu.VMEM((energy_rows, LANES), jnp.float32),
            pltpu.VMEM((templ * local, LANES), jnp.int32),
            pltpu.VMEM((8, LANES), jnp.float32),
            pltpu.VMEM((len(LEVELS), 2 * CHUNK, LANES), jnp.bfloat16),
            pltpu.VMEM((n, rows, OUT), jnp.float32),
            pltpu.VMEM((n, rows, OUT), jnp.float32),
            pltpu.SemaphoreType.DMA((4,)),
            pltpu.SemaphoreType.DMA,
            pltpu.SemaphoreType.DMA,
            pltpu.SemaphoreType.REGULAR,
        ],
        compiler_params=pltpu.CompilerParams(collective_id=0, vmem_limit_bytes=16 << 20, has_side_effects=True),
    )(*[
        pltpu.with_memory_space_constraint(x, pltpu.HBM) for x in (records, templates, shifts, present)])


def solution(mesh):
    placed = (P("sta", None, "parts"), P(None, "sta", None, None), P(), P())
    return jax.shard_map(
        body, mesh=mesh, in_specs=placed, out_specs=P("sta", "parts"), check_vma=False
    )
```

```python
import functools
import math

import jax
import jax.numpy as jnp
from jax import lax
from jax.experimental import pallas as pl
from jax.experimental.pallas import tpu as pltpu
from jax.sharding import PartitionSpec as P

LEN = 600
WIN = 640
MAXSHIFT = 512
OUT = WIN - MAXSHIFT
LANES = 128
SUB = 16
GROUPS = LANES // SUB
TAPS = -(-LEN // LANES)
LAGS = WIN + LANES
WIDE = WIN + TAPS * LANES
FULL, REST = divmod(LEN, LANES)
CHUNK = 8
LEVELS = (7,)


def transposed(tiles, part_v):
    for level, bits in enumerate(LEVELS):
        parts = part_v[level]
        moves = [m for m in range(GROUPS) if m & bits == m]
        out = []
        for i in range(GROUPS):
            mixed = None
            for m in moves:
                x = tiles[i & ~bits | m]
                turn = SUB * (m - (i & bits)) % LANES
                x = pltpu.roll(x, turn, 1) if turn else x
                mixed = x if mixed is None else jnp.where(parts == m, x, mixed)
            out.append(mixed)
        tiles = out
    return tiles


def kernel(
    n, rec_hbm, tem_hbm, shift_hbm, present_hbm, out_ref,
    rec_in, tem_in, tem, shift_v, present_s, rec, hank, energy, band, sums, inv_v, lag_v, pair, part_v, total, recv,
    in_sem, send_sem, recv_sem, ready_sem,
):
    me = lax.axis_index("sta")
    templ, local = tem_in.shape[0], tem_in.shape[2]
    rows = templ // n
    samples = rec_in.shape[2]
    stations = n * local

    def load(src, dst, i):
        return pltpu.make_async_copy(src, dst, in_sem.at[i])

    def tem_load(start, count, i):
        return load(tem_hbm.at[pl.ds(start, count)], tem_in.at[pl.ds(start, count)], i)

    rec_load = pltpu.make_async_copy(rec_hbm, rec_in, send_sem)
    shift_load = load(shift_hbm, shift_v, 0)
    present_load = load(present_hbm, present_s, 1)
    small = 8 // local
    first = tem_load(0, small, 2)
    others = tem_load(small, templ - small, 3)
    for x in [first, rec_load, shift_load, present_load, others]:
        x.start()

    barrier = pltpu.get_barrier_semaphore()

    def greet(d, carry):
        pl.semaphore_signal(barrier, inc=1, device_id={"sta": d}, device_id_type=pl.DeviceIdType.MESH)
        return carry

    def answer(d, carry):
        pl.semaphore_signal(
            ready_sem, inc=1, device_id={"sta": d}, device_id_type=pl.DeviceIdType.MESH
        )
        return carry

    lax.fori_loop(me + 1, n, greet, 0)

    @pl.when(me > 0)
    def _():
        pl.semaphore_wait(barrier, me)


    at = lax.broadcasted_iota(jnp.int32, (LANES, LANES), 0)
    to = lax.broadcasted_iota(jnp.int32, (LANES, LANES), 1)
    for i, mask in enumerate([at >= to, at >= 0, at < to + REST, at < to + (REST - LANES)]):
        band[:, i * LANES : (i + 1) * LANES] = mask.astype(jnp.float32).astype(jnp.bfloat16)
    energy[...] = jnp.zeros_like(energy)
    rec[...] = jnp.zeros_like(rec)
    for c in range(3):
        tem[c * TAPS + FULL] = jnp.zeros((templ * local, LANES), tem.dtype)
    lane = lax.broadcasted_iota(jnp.int32, (CHUNK, LANES), 1)
    block = lax.broadcasted_iota(jnp.int32, (2 * CHUNK, LANES), 1) // SUB

    for level, bits in enumerate(LEVELS):
        part_v[level] = (block & bits).astype(jnp.float32).astype(jnp.bfloat16)

    for x in [rec_load, shift_load, present_load, first]:
        x.wait()
    waves = [rec_in[c].astype(jnp.float32) for c in range(3)]
    for c in range(3):
        rec[c * local : (c + 1) * local, 0:samples] = waves[c]
    power = waves[0] * waves[0] + waves[1] * waves[1] + waves[2] * waves[2]
    for q in range(-(-samples // LANES)):
        span = min(LANES, samples - q * LANES)
        energy[q * local : (q + 1) * local, 0:span] = power[:, q * LANES : q * LANES + span]
    flip = 7 - lax.broadcasted_iota(jnp.int32, (8, LANES), 0)
    for s in range(local):
        for c in range(3):
            row = jnp.broadcast_to(rec[c * local + s : c * local + s + 1, :], (SUB, WIDE))
            slid = pltpu.roll(row, WIDE - SUB + 1, 1, stride=1, stride_axis=0)
            for i in range(0, WIDE, LANES):
                hank[s, c, :, i : i + LANES] = jnp.concatenate(
                    [jnp.take_along_axis(slid[r : r + 8, i : i + LANES], flip, axis=0) for r in (8, 0)], axis=0
                ).astype(jnp.bfloat16)

    whole = energy[...]
    count = whole.shape[0]
    high = whole.astype(jnp.bfloat16)
    left = whole - high.astype(jnp.float32)
    middle = left.astype(jnp.bfloat16)
    low = (left - middle.astype(jnp.float32)).astype(jnp.bfloat16)
    split = jnp.dot(
        jnp.concatenate([high, middle, low], axis=0), band[...], preferred_element_type=jnp.float32
    )
    sums[...] = split[:count] + split[count : 2 * count] + split[2 * count :]
    lag_rows = local * (WIN // LANES)

    def part(kind, behind):
        return sums[behind * local : behind * local + lag_rows, kind * LANES : (kind + 1) * LANES]

    window = part(0, 0) + part(2, FULL) + part(3, FULL + 1)
    for i in range(1, FULL):
        window = window + part(1, i)
    inv_v[0:lag_rows, :] = lax.rsqrt(window / (3 * LEN) + 1e-06)

    def inverse(s):
        return [
            jnp.broadcast_to(inv_v[i * local + s : i * local + s + 1, :], (CHUNK, LANES))
            for i in range(WIN // LANES)
        ]


    lags_all = shift_v[...].astype(jnp.float32)
    column = lax.broadcasted_iota(jnp.int32, lags_all.shape, 1)
    scale = math.sqrt(3 * LEN / stations) / (3 * LEN)
    flags = []
    for s in range(local):
        lag = jnp.sum(jnp.where(column == me * local + s, lags_all, 0.0), axis=1, keepdims=True)
        lag_v[pl.ds(s, templ, stride=local), :] = jnp.broadcast_to(lag.astype(jnp.int32), (templ, LANES))
        flags.append(present_s[me * local + s].astype(jnp.float32) * scale)

    which = lax.broadcasted_iota(jnp.int32, (8, LANES), 0) % local

    def by_station(values):
        out = values[0]
        for s in range(1, local):
            out = jnp.where(which == s, values[s], out)
        return out

    def picked(tiles, pos):
        coarse, fine = pos >> (LANES.bit_length() - 1), pos & (LANES - 1)
        near, far = tiles[0], tiles[1]
        for i in range(1, len(tiles) - 1):
            near = jnp.where(coarse == i, tiles[i], near)
            far = jnp.where(coarse == i, tiles[i + 1], far)
        return jnp.take_along_axis(
            jnp.where(lane >= fine, near, far), (lane + fine) & (LANES - 1), axis=1
        )

    def stage(t0, count):
        for t in range(t0, t0 + count):
            for c in range(3):
                wave = tem_in[t, c].astype(jnp.float32)
                for a in range(TAPS):
                    span = min(LANES, LEN - a * LANES)
                    tem[c * TAPS + a, t * local : (t + 1) * local, 0:span] = wave[:, a * LANES : a * LANES + span]

    def operands(tiles):
        square = sum(x * x for x in tiles)
        gain = lax.rsqrt(jnp.sum(square, axis=1, keepdims=True) / (3 * LEN) + 1e-06)
        tiles = tiles + [jnp.zeros((8, LANES), jnp.float32)] * (2 * GROUPS - len(tiles))
        pairs = [
            jnp.concatenate([tiles[i], tiles[i + GROUPS]], axis=0).astype(jnp.bfloat16)
            for i in range(GROUPS)
        ]
        pairs = [x.astype(jnp.float32) for x in transposed(pairs, part_v)]
        left = jnp.concatenate([jnp.concatenate([x[:8], x[8:]], axis=1) for x in pairs], axis=0)
        return gain, left[:, : 3 * TAPS * SUB].astype(jnp.bfloat16)

    def raw(left, s):
        right = jnp.concatenate(
            [hank[s, c, :, a * LANES : a * LANES + LAGS] for c in range(3) for a in range(TAPS)], axis=0
        )
        both = jnp.dot(left, right, preferred_element_type=jnp.float32)
        return [
            [both[j * 8 : j * 8 + 8, i * LANES : (i + 1) * LANES] for i in range(LAGS // LANES)]
            for j in range(GROUPS)
        ]

    def keep(done, t0):
        for i in range(done.shape[0] // rows):
            total[t0 // rows + i] = done[i * rows : (i + 1) * rows]

    def stacked(parts, lag, window):
        acc = sum(picked(parts[j], lag + j * SUB) for j in range(GROUPS))
        return acc * picked(window + [window[-1]], lag)

    def work_small(t0):
        count = 8 // local
        stage(t0, count)
        first = t0 * local
        gain, left = operands([tem[i, first : first + 8, :] for i in range(3 * TAPS)])
        raws = [raw(left, s) for s in range(local)]
        parts = [
            [by_station([r[j][i] for r in raws]) for i in range(LAGS // LANES)] for j in range(GROUPS)
        ]
        window = [by_station(list(x)) for x in zip(*[inverse(s) for s in range(local)])]
        flag = by_station([jnp.full((8, LANES), f) for f in flags])
        pair[...] = stacked(parts, lag_v[first : first + 8, :], window) * (gain * flag)
        keep(sum(pair[pl.ds(s, count, stride=local), :] for s in range(local)), t0)

    def work(t0):
        stage(t0, CHUNK)
        done = jnp.zeros((CHUNK, LANES), jnp.float32)
        for s in range(local):
            mine = pl.ds(t0 * local + s, CHUNK, stride=local)
            gain, left = operands([tem[i, mine, :] for i in range(3 * TAPS)])
            done = done + stacked(raw(left, s), lag_v[mine, :], inverse(s)) * (gain * flags[s])
        keep(done, t0)

    def send(d):
        pltpu.make_async_remote_copy(
            src_ref=total.at[d], dst_ref=recv.at[lax.rem(d - me + n, n)],
            send_sem=send_sem, recv_sem=recv_sem,
            device_id={"sta": d}, device_id_type=pl.DeviceIdType.MESH,
        ).start()

    def send_back(t0, count):
        for d in range(t0 // rows, (t0 + count) // rows):

            @pl.when(d < me)
            def _():
                send(d)

    def send_on(d, carry):
        send(d)
        return carry

    work_small(0)
    send_back(0, small)
    lax.fori_loop(0, me, answer, 0)
    others.wait()
    for t0 in range(small, CHUNK, small):
        work_small(t0)
        send_back(t0, small)
    for t0 in range(CHUNK, templ, CHUNK):
        work(t0)
        send_back(t0, CHUNK)

    @pl.when(me < n - 1)
    def _():
        pl.semaphore_wait(ready_sem, n - 1 - me)

    lax.fori_loop(me + 1, n, send_on, 0)
    rest = recv.at[pl.ds(1, n - 1)]
    pltpu.make_async_copy(rest, rest, recv_sem).wait()
    pltpu.make_async_copy(rest, rest, send_sem).wait()
    out_ref[...] = total[me] + jnp.sum(recv[pl.ds(1, n - 1)], axis=0)


def body(records, templates, shifts, present):
    n = lax.axis_size("sta")
    templ, local = templates.shape[0], templates.shape[1]
    rows = templ // n
    records = records.transpose(1, 0, 2)
    templates = templates.transpose(0, 2, 1, 3)
    energy_rows = -(-local * (WIDE // LANES) // 16) * 16
    hbm = pl.BlockSpec(memory_space=pl.ANY)
    return pl.pallas_call(
        functools.partial(kernel, n),
        out_shape=jax.ShapeDtypeStruct((rows, OUT), jnp.float32),
        in_specs=[hbm] * 4,
        out_specs=pl.BlockSpec(memory_space=pltpu.VMEM),
        scratch_shapes=[
            pltpu.VMEM(records.shape, records.dtype),
            pltpu.VMEM(templates.shape, templates.dtype),
            pltpu.VMEM((3 * TAPS, templ * local, LANES), jnp.float32),
            pltpu.VMEM(shifts.shape, shifts.dtype),
            pltpu.SMEM(present.shape, present.dtype),
            pltpu.VMEM((-(-3 * local // 8) * 8, WIDE), jnp.float32),
            pltpu.VMEM((local, 3, SUB, WIDE), jnp.bfloat16),
            pltpu.VMEM((energy_rows, LANES), jnp.float32),
            pltpu.VMEM((LANES, 4 * LANES), jnp.bfloat16),
            pltpu.VMEM((energy_rows, 4 * LANES), jnp.float32),
            pltpu.VMEM((energy_rows, LANES), jnp.float32),
            pltpu.VMEM((templ * local, LANES), jnp.int32),
            pltpu.VMEM((8, LANES), jnp.float32),
            pltpu.VMEM((len(LEVELS), 2 * CHUNK, LANES), jnp.bfloat16),
            pltpu.VMEM((n, rows, OUT), jnp.float32),
            pltpu.VMEM((n, rows, OUT), jnp.float32),
            pltpu.SemaphoreType.DMA((4,)),
            pltpu.SemaphoreType.DMA,
            pltpu.SemaphoreType.DMA,
            pltpu.SemaphoreType.REGULAR,
        ],
        compiler_params=pltpu.CompilerParams(collective_id=0, vmem_limit_bytes=16 << 20, has_side_effects=True),
    )(*[
        pltpu.with_memory_space_constraint(x, pltpu.HBM) for x in (records, templates, shifts, present)])


def solution(mesh):
    placed = (P("sta", None, "parts"), P(None, "sta", None, None), P(), P())
    return jax.shard_map(
        body, mesh=mesh, in_specs=placed, out_specs=P("sta", "parts"), check_vma=False
    )
```

```python
import functools
import math

import jax
import jax.numpy as jnp
from jax import lax
from jax.experimental import pallas as pl
from jax.experimental.pallas import tpu as pltpu
from jax.sharding import PartitionSpec as P

LEN = 600
WIN = 640
MAXSHIFT = 512
OUT = WIN - MAXSHIFT
LANES = 128
SUB = 16
GROUPS = LANES // SUB
TAPS = -(-LEN // LANES)
LAGS = WIN + LANES
WIDE = WIN + TAPS * LANES
FULL, REST = divmod(LEN, LANES)
CHUNK = 8
LEVELS = (7,)


def transposed(tiles, part_v):
    for level, bits in enumerate(LEVELS):
        parts = part_v[level]
        moves = [m for m in range(GROUPS) if m & bits == m]
        out = []
        for i in range(GROUPS):
            mixed = None
            for m in moves:
                x = tiles[i & ~bits | m]
                turn = SUB * (m - (i & bits)) % LANES
                x = pltpu.roll(x, turn, 1) if turn else x
                mixed = x if mixed is None else jnp.where(parts == m, x, mixed)
            out.append(mixed)
        tiles = out
    return tiles


def kernel(
    n, rec_hbm, tem_hbm, shift_hbm, present_hbm, out_ref,
    rec_in, tem_in, tem, shift_v, present_s, rec, hank, energy, band, sums, inv_v, lag_v, pair, part_v, total, recv,
    in_sem, send_sem, recv_sem,
):
    me = lax.axis_index("sta")
    templ, local = tem_in.shape[0], tem_in.shape[2]
    rows = templ // n
    samples = rec_in.shape[2]
    stations = n * local

    def load(src, dst, i):
        return pltpu.make_async_copy(src, dst, in_sem.at[i])

    def tem_load(start, count, i):
        return load(tem_hbm.at[pl.ds(start, count)], tem_in.at[pl.ds(start, count)], i)

    rec_load = pltpu.make_async_copy(rec_hbm, rec_in, send_sem)
    shift_load = load(shift_hbm, shift_v, 0)
    present_load = load(present_hbm, present_s, 1)
    small = 8 // local
    first = tem_load(0, small, 2)
    others = tem_load(small, templ - small, 3)
    for x in [first, rec_load, shift_load, present_load, others]:
        x.start()

    barrier = pltpu.get_barrier_semaphore()

    for step in range(1, n):
        pl.semaphore_signal(
            barrier, inc=1, device_id={"sta": lax.rem(me + step, n)},
            device_id_type=pl.DeviceIdType.MESH,
        )
    late = me >= n // 2

    at = lax.broadcasted_iota(jnp.int32, (LANES, LANES), 0)
    to = lax.broadcasted_iota(jnp.int32, (LANES, LANES), 1)
    for i, mask in enumerate([at >= to, at >= 0, at < to + REST, at < to + (REST - LANES)]):
        band[:, i * LANES : (i + 1) * LANES] = mask.astype(jnp.float32).astype(jnp.bfloat16)
    energy[...] = jnp.zeros_like(energy)
    rec[...] = jnp.zeros_like(rec)
    for c in range(3):
        tem[c * TAPS + FULL] = jnp.zeros((templ * local, LANES), tem.dtype)
    lane = lax.broadcasted_iota(jnp.int32, (CHUNK, LANES), 1)
    block = lax.broadcasted_iota(jnp.int32, (2 * CHUNK, LANES), 1) // SUB

    for level, bits in enumerate(LEVELS):
        part_v[level] = (block & bits).astype(jnp.float32).astype(jnp.bfloat16)

    for x in [rec_load, shift_load, present_load, first]:
        x.wait()
    waves = [rec_in[c].astype(jnp.float32) for c in range(3)]
    for c in range(3):
        rec[c * local : (c + 1) * local, 0:samples] = waves[c]
    power = waves[0] * waves[0] + waves[1] * waves[1] + waves[2] * waves[2]
    for q in range(-(-samples // LANES)):
        span = min(LANES, samples - q * LANES)
        energy[q * local : (q + 1) * local, 0:span] = power[:, q * LANES : q * LANES + span]
    flip = 7 - lax.broadcasted_iota(jnp.int32, (8, LANES), 0)
    for s in range(local):
        for c in range(3):
            row = jnp.broadcast_to(rec[c * local + s : c * local + s + 1, :], (SUB, WIDE))
            slid = pltpu.roll(row, WIDE - SUB + 1, 1, stride=1, stride_axis=0)
            for i in range(0, WIDE, LANES):
                hank[s, c, :, i : i + LANES] = jnp.concatenate(
                    [jnp.take_along_axis(slid[r : r + 8, i : i + LANES], flip, axis=0) for r in (8, 0)], axis=0
                ).astype(jnp.bfloat16)

    whole = energy[...]
    count = whole.shape[0]
    high = whole.astype(jnp.bfloat16)
    left = whole - high.astype(jnp.float32)
    middle = left.astype(jnp.bfloat16)
    low = (left - middle.astype(jnp.float32)).astype(jnp.bfloat16)
    split = jnp.dot(
        jnp.concatenate([high, middle, low], axis=0), band[...], preferred_element_type=jnp.float32
    )
    sums[...] = split[:count] + split[count : 2 * count] + split[2 * count :]
    lag_rows = local * (WIN // LANES)

    def part(kind, behind):
        return sums[behind * local : behind * local + lag_rows, kind * LANES : (kind + 1) * LANES]

    window = part(0, 0) + part(2, FULL) + part(3, FULL + 1)
    for i in range(1, FULL):
        window = window + part(1, i)
    inv_v[0:lag_rows, :] = lax.rsqrt(window / (3 * LEN) + 1e-06)

    def inverse(s):
        return [
            jnp.broadcast_to(inv_v[i * local + s : i * local + s + 1, :], (CHUNK, LANES))
            for i in range(WIN // LANES)
        ]


    lags_all = shift_v[...].astype(jnp.float32)
    column = lax.broadcasted_iota(jnp.int32, lags_all.shape, 1)
    scale = math.sqrt(3 * LEN / stations) / (3 * LEN)
    flags = []
    for s in range(local):
        lag = jnp.sum(jnp.where(column == me * local + s, lags_all, 0.0), axis=1, keepdims=True)
        lag_v[pl.ds(s, templ, stride=local), :] = jnp.broadcast_to(lag.astype(jnp.int32), (templ, LANES))
        flags.append(present_s[me * local + s].astype(jnp.float32) * scale)

    which = lax.broadcasted_iota(jnp.int32, (8, LANES), 0) % local

    def by_station(values):
        out = values[0]
        for s in range(1, local):
            out = jnp.where(which == s, values[s], out)
        return out

    def picked(tiles, pos):
        coarse, fine = pos >> (LANES.bit_length() - 1), pos & (LANES - 1)
        near, far = tiles[0], tiles[1]
        for i in range(1, len(tiles) - 1):
            near = jnp.where(coarse == i, tiles[i], near)
            far = jnp.where(coarse == i, tiles[i + 1], far)
        return jnp.take_along_axis(
            jnp.where(lane >= fine, near, far), (lane + fine) & (LANES - 1), axis=1
        )

    def stage(t0, count):
        for t in range(t0, t0 + count):
            for c in range(3):
                wave = tem_in[t, c].astype(jnp.float32)
                for a in range(TAPS):
                    span = min(LANES, LEN - a * LANES)
                    tem[c * TAPS + a, t * local : (t + 1) * local, 0:span] = wave[:, a * LANES : a * LANES + span]

    def operands(tiles):
        square = sum(x * x for x in tiles)
        gain = lax.rsqrt(jnp.sum(square, axis=1, keepdims=True) / (3 * LEN) + 1e-06)
        tiles = tiles + [jnp.zeros((8, LANES), jnp.float32)] * (2 * GROUPS - len(tiles))
        pairs = [
            jnp.concatenate([tiles[i], tiles[i + GROUPS]], axis=0).astype(jnp.bfloat16)
            for i in range(GROUPS)
        ]
        pairs = [x.astype(jnp.float32) for x in transposed(pairs, part_v)]
        left = jnp.concatenate([jnp.concatenate([x[:8], x[8:]], axis=1) for x in pairs], axis=0)
        return gain, left[:, : 3 * TAPS * SUB].astype(jnp.bfloat16)

    def raw(left, s):
        right = jnp.concatenate(
            [hank[s, c, :, a * LANES : a * LANES + LAGS] for c in range(3) for a in range(TAPS)], axis=0
        )
        both = jnp.dot(left, right, preferred_element_type=jnp.float32)
        return [
            [both[j * 8 : j * 8 + 8, i * LANES : (i + 1) * LANES] for i in range(LAGS // LANES)]
            for j in range(GROUPS)
        ]

    def keep(done, t0):
        for i in range(done.shape[0] // rows):
            total[t0 // rows + i] = done[i * rows : (i + 1) * rows]

    def stacked(parts, lag, window):
        acc = sum(picked(parts[j], lag + j * SUB) for j in range(GROUPS))
        return acc * picked(window + [window[-1]], lag)

    def work_small(t0):
        count = 8 // local
        stage(t0, count)
        first = t0 * local
        gain, left = operands([tem[i, first : first + 8, :] for i in range(3 * TAPS)])
        raws = [raw(left, s) for s in range(local)]
        parts = [
            [by_station([r[j][i] for r in raws]) for i in range(LAGS // LANES)] for j in range(GROUPS)
        ]
        window = [by_station(list(x)) for x in zip(*[inverse(s) for s in range(local)])]
        flag = by_station([jnp.full((8, LANES), f) for f in flags])
        pair[...] = stacked(parts, lag_v[first : first + 8, :], window) * (gain * flag)
        keep(sum(pair[pl.ds(s, count, stride=local), :] for s in range(local)), t0)

    def work(t0):
        stage(t0, CHUNK)
        done = jnp.zeros((CHUNK, LANES), jnp.float32)
        for s in range(local):
            mine = pl.ds(t0 * local + s, CHUNK, stride=local)
            gain, left = operands([tem[i, mine, :] for i in range(3 * TAPS)])
            done = done + stacked(raw(left, s), lag_v[mine, :], inverse(s)) * (gain * flags[s])
        keep(done, t0)

    def send(d):
        pltpu.make_async_remote_copy(
            src_ref=total.at[d], dst_ref=recv.at[lax.rem(d - me + n, n)],
            send_sem=send_sem, recv_sem=recv_sem,
            device_id={"sta": d}, device_id_type=pl.DeviceIdType.MESH,
        ).start()

    def send_early(t0, count):
        for d in range(t0 // rows, (t0 + count) // rows):

            @pl.when(jnp.logical_and(late, me != d))
            def _():
                send(d)

    def send_on(d, carry):
        send(d)
        return carry

    work_small(0)

    @pl.when(late)
    def _():
        pl.semaphore_wait(barrier, n - 1)

    send_early(0, small)
    others.wait()
    for t0 in range(small, CHUNK, small):
        work_small(t0)
        send_early(t0, small)
    for t0 in range(CHUNK, templ, CHUNK):
        work(t0)
        send_early(t0, CHUNK)

    @pl.when(jnp.logical_not(late))
    def _():
        pl.semaphore_wait(barrier, n - 1)
        lax.fori_loop(0, me, send_on, 0)
        lax.fori_loop(me + 1, n, send_on, 0)

    rest = recv.at[pl.ds(1, n - 1)]
    pltpu.make_async_copy(rest, rest, recv_sem).wait()
    pltpu.make_async_copy(rest, rest, send_sem).wait()
    out_ref[...] = total[me] + jnp.sum(recv[pl.ds(1, n - 1)], axis=0)


def body(records, templates, shifts, present):
    n = lax.axis_size("sta")
    templ, local = templates.shape[0], templates.shape[1]
    rows = templ // n
    records = records.transpose(1, 0, 2)
    templates = templates.transpose(0, 2, 1, 3)
    energy_rows = -(-local * (WIDE // LANES) // 16) * 16
    hbm = pl.BlockSpec(memory_space=pl.ANY)
    return pl.pallas_call(
        functools.partial(kernel, n),
        out_shape=jax.ShapeDtypeStruct((rows, OUT), jnp.float32),
        in_specs=[hbm] * 4,
        out_specs=pl.BlockSpec(memory_space=pltpu.VMEM),
        scratch_shapes=[
            pltpu.VMEM(records.shape, records.dtype),
            pltpu.VMEM(templates.shape, templates.dtype),
            pltpu.VMEM((3 * TAPS, templ * local, LANES), jnp.float32),
            pltpu.VMEM(shifts.shape, shifts.dtype),
            pltpu.SMEM(present.shape, present.dtype),
            pltpu.VMEM((-(-3 * local // 8) * 8, WIDE), jnp.float32),
            pltpu.VMEM((local, 3, SUB, WIDE), jnp.bfloat16),
            pltpu.VMEM((energy_rows, LANES), jnp.float32),
            pltpu.VMEM((LANES, 4 * LANES), jnp.bfloat16),
            pltpu.VMEM((energy_rows, 4 * LANES), jnp.float32),
            pltpu.VMEM((energy_rows, LANES), jnp.float32),
            pltpu.VMEM((templ * local, LANES), jnp.int32),
            pltpu.VMEM((8, LANES), jnp.float32),
            pltpu.VMEM((len(LEVELS), 2 * CHUNK, LANES), jnp.bfloat16),
            pltpu.VMEM((n, rows, OUT), jnp.float32),
            pltpu.VMEM((n, rows, OUT), jnp.float32),
            pltpu.SemaphoreType.DMA((4,)),
            pltpu.SemaphoreType.DMA,
            pltpu.SemaphoreType.DMA,
        ],
        compiler_params=pltpu.CompilerParams(collective_id=0, vmem_limit_bytes=16 << 20, has_side_effects=True),
    )(*[
        pltpu.with_memory_space_constraint(x, pltpu.HBM) for x in (records, templates, shifts, present)])


def solution(mesh):
    placed = (P("sta", None, "parts"), P(None, "sta", None, None), P(), P())
    return jax.shard_map(
        body, mesh=mesh, in_specs=placed, out_specs=P("sta", "parts"), check_vma=False
    )
```

```python
import functools
import math

import jax
import jax.numpy as jnp
from jax import lax
from jax.experimental import pallas as pl
from jax.experimental.pallas import tpu as pltpu
from jax.sharding import PartitionSpec as P

LEN = 600
WIN = 640
MAXSHIFT = 512
OUT = WIN - MAXSHIFT
LANES = 128
SUB = 16
GROUPS = LANES // SUB
TAPS = -(-LEN // LANES)
LAGS = WIN + LANES
WIDE = WIN + TAPS * LANES
FULL, REST = divmod(LEN, LANES)
CHUNK = 8
LEVELS = (7,)


def transposed(tiles, part_v):
    for level, bits in enumerate(LEVELS):
        parts = part_v[level]
        moves = [m for m in range(GROUPS) if m & bits == m]
        out = []
        for i in range(GROUPS):
            mixed = None
            for m in moves:
                x = tiles[i & ~bits | m]
                turn = SUB * (m - (i & bits)) % LANES
                x = pltpu.roll(x, turn, 1) if turn else x
                mixed = x if mixed is None else jnp.where(parts == m, x, mixed)
            out.append(mixed)
        tiles = out
    return tiles


def kernel(
    n, rec_hbm, tem_hbm, shift_hbm, present_hbm, out_ref,
    rec_in, tem_in, tem, shift_v, present_s, rec, hank, energy, band, sums, inv_v, lag_v, pair, part_v, total, recv,
    in_sem, send_sem, recv_sem,
):
    me = lax.axis_index("sta")
    templ, local = tem_in.shape[0], tem_in.shape[2]
    rows = templ // n
    samples = rec_in.shape[2]
    stations = n * local

    def load(src, dst, i):
        return pltpu.make_async_copy(src, dst, in_sem.at[i])

    def tem_load(start, count, i):
        return load(tem_hbm.at[pl.ds(start, count)], tem_in.at[pl.ds(start, count)], i)

    rec_load = pltpu.make_async_copy(rec_hbm, rec_in, send_sem)
    shift_load = load(shift_hbm, shift_v, 0)
    present_load = load(present_hbm, present_s, 1)
    small = 8 // local
    first = tem_load(0, small, 2)
    others = tem_load(small, templ - small, 3)
    for x in [first, rec_load, shift_load, present_load, others]:
        x.start()

    barrier = pltpu.get_barrier_semaphore()

    for step in range(1, n):
        pl.semaphore_signal(
            barrier, inc=1, device_id={"sta": lax.rem(me + step, n)},
            device_id_type=pl.DeviceIdType.MESH,
        )
    late = me >= n // 2

    at = lax.broadcasted_iota(jnp.int32, (LANES, LANES), 0)
    to = lax.broadcasted_iota(jnp.int32, (LANES, LANES), 1)
    for i, mask in enumerate([at >= to, at >= 0, at < to + REST, at < to + (REST - LANES)]):
        band[:, i * LANES : (i + 1) * LANES] = mask.astype(jnp.float32).astype(jnp.bfloat16)
    energy[...] = jnp.zeros_like(energy)
    rec[...] = jnp.zeros_like(rec)
    for c in range(3):
        tem[c * TAPS + FULL] = jnp.zeros((templ * local, LANES), tem.dtype)
    lane = lax.broadcasted_iota(jnp.int32, (CHUNK, LANES), 1)
    block = lax.broadcasted_iota(jnp.int32, (2 * CHUNK, LANES), 1) // SUB

    for level, bits in enumerate(LEVELS):
        part_v[level] = (block & bits).astype(jnp.float32).astype(jnp.bfloat16)

    for x in [rec_load, shift_load, present_load, first]:
        x.wait()
    waves = [rec_in[c].astype(jnp.float32) for c in range(3)]
    for c in range(3):
        rec[c * local : (c + 1) * local, 0:samples] = waves[c]
    power = waves[0] * waves[0] + waves[1] * waves[1] + waves[2] * waves[2]
    for q in range(-(-samples // LANES)):
        span = min(LANES, samples - q * LANES)
        energy[q * local : (q + 1) * local, 0:span] = power[:, q * LANES : q * LANES + span]
    flip = 7 - lax.broadcasted_iota(jnp.int32, (8, LANES), 0)
    for s in range(local):
        for c in range(3):
            row = jnp.broadcast_to(rec[c * local + s : c * local + s + 1, :], (SUB, WIDE))
            slid = pltpu.roll(row, WIDE - SUB + 1, 1, stride=1, stride_axis=0)
            for i in range(0, WIDE, LANES):
                hank[s, c, :, i : i + LANES] = jnp.concatenate(
                    [jnp.take_along_axis(slid[r : r + 8, i : i + LANES], flip, axis=0) for r in (8, 0)], axis=0
                ).astype(jnp.bfloat16)

    whole = energy[...]
    count = whole.shape[0]
    high = whole.astype(jnp.bfloat16)
    left = whole - high.astype(jnp.float32)
    middle = left.astype(jnp.bfloat16)
    low = (left - middle.astype(jnp.float32)).astype(jnp.bfloat16)
    split = jnp.dot(
        jnp.concatenate([high, middle, low], axis=0), band[...], preferred_element_type=jnp.float32
    )
    sums[...] = split[:count] + split[count : 2 * count] + split[2 * count :]
    lag_rows = local * (WIN // LANES)

    def part(kind, behind):
        return sums[behind * local : behind * local + lag_rows, kind * LANES : (kind + 1) * LANES]

    window = part(0, 0) + part(2, FULL) + part(3, FULL + 1)
    for i in range(1, FULL):
        window = window + part(1, i)
    inv_v[0:lag_rows, :] = lax.rsqrt(window / (3 * LEN) + 1e-06)

    def inverse(s):
        return [
            jnp.broadcast_to(inv_v[i * local + s : i * local + s + 1, :], (CHUNK, LANES))
            for i in range(WIN // LANES)
        ]


    lags_all = shift_v[...].astype(jnp.float32)
    column = lax.broadcasted_iota(jnp.int32, lags_all.shape, 1)
    scale = math.sqrt(3 * LEN / stations) / (3 * LEN)
    flags = []
    for s in range(local):
        lag = jnp.sum(jnp.where(column == me * local + s, lags_all, 0.0), axis=1, keepdims=True)
        lag_v[pl.ds(s, templ, stride=local), :] = jnp.broadcast_to(lag.astype(jnp.int32), (templ, LANES))
        flags.append(present_s[me * local + s].astype(jnp.float32) * scale)

    which = lax.broadcasted_iota(jnp.int32, (8, LANES), 0) % local

    def by_station(values):
        out = values[0]
        for s in range(1, local):
            out = jnp.where(which == s, values[s], out)
        return out

    def picked(tiles, pos):
        coarse, fine = pos >> (LANES.bit_length() - 1), pos & (LANES - 1)
        near, far = tiles[0], tiles[1]
        for i in range(1, len(tiles) - 1):
            near = jnp.where(coarse == i, tiles[i], near)
            far = jnp.where(coarse == i, tiles[i + 1], far)
        return jnp.take_along_axis(
            jnp.where(lane >= fine, near, far), (lane + fine) & (LANES - 1), axis=1
        )

    def stage(t0, count):
        for t in range(t0, t0 + count):
            for c in range(3):
                wave = tem_in[t, c].astype(jnp.float32)
                for a in range(TAPS):
                    span = min(LANES, LEN - a * LANES)
                    tem[c * TAPS + a, t * local : (t + 1) * local, 0:span] = wave[:, a * LANES : a * LANES + span]

    def operands(tiles):
        square = sum(x * x for x in tiles)
        gain = lax.rsqrt(jnp.sum(square, axis=1, keepdims=True) / (3 * LEN) + 1e-06)
        tiles = tiles + [jnp.zeros((8, LANES), jnp.float32)] * (2 * GROUPS - len(tiles))
        pairs = [
            jnp.concatenate([tiles[i], tiles[i + GROUPS]], axis=0).astype(jnp.bfloat16)
            for i in range(GROUPS)
        ]
        pairs = [x.astype(jnp.float32) for x in transposed(pairs, part_v)]
        left = jnp.concatenate([jnp.concatenate([x[:8], x[8:]], axis=1) for x in pairs], axis=0)
        return gain, left.astype(jnp.bfloat16)

    def raw(left, s):
        right = jnp.concatenate(
            [hank[s, c, :, a * LANES : a * LANES + LAGS] for c in range(3) for a in range(TAPS)]
            + [jnp.zeros((2 * LANES - 3 * TAPS * SUB, LAGS), jnp.bfloat16)],
            axis=0,
        )
        both = jnp.dot(left, right, preferred_element_type=jnp.float32)
        return [
            [both[j * 8 : j * 8 + 8, i * LANES : (i + 1) * LANES] for i in range(LAGS // LANES)]
            for j in range(GROUPS)
        ]

    def keep(done, t0):
        for i in range(done.shape[0] // rows):
            total[t0 // rows + i] = done[i * rows : (i + 1) * rows]

    def stacked(parts, lag, window):
        acc = sum(picked(parts[j], lag + j * SUB) for j in range(GROUPS))
        return acc * picked(window + [window[-1]], lag)

    def work_small(t0):
        count = 8 // local
        stage(t0, count)
        first = t0 * local
        gain, left = operands([tem[i, first : first + 8, :] for i in range(3 * TAPS)])
        raws = [raw(left, s) for s in range(local)]
        parts = [
            [by_station([r[j][i] for r in raws]) for i in range(LAGS // LANES)] for j in range(GROUPS)
        ]
        window = [by_station(list(x)) for x in zip(*[inverse(s) for s in range(local)])]
        flag = by_station([jnp.full((8, LANES), f) for f in flags])
        pair[...] = stacked(parts, lag_v[first : first + 8, :], window) * (gain * flag)
        keep(sum(pair[pl.ds(s, count, stride=local), :] for s in range(local)), t0)

    def work(t0):
        stage(t0, CHUNK)
        done = jnp.zeros((CHUNK, LANES), jnp.float32)
        for s in range(local):
            mine = pl.ds(t0 * local + s, CHUNK, stride=local)
            gain, left = operands([tem[i, mine, :] for i in range(3 * TAPS)])
            done = done + stacked(raw(left, s), lag_v[mine, :], inverse(s)) * (gain * flags[s])
        keep(done, t0)

    def send(d):
        pltpu.make_async_remote_copy(
            src_ref=total.at[d], dst_ref=recv.at[lax.rem(d - me + n, n)],
            send_sem=send_sem, recv_sem=recv_sem,
            device_id={"sta": d}, device_id_type=pl.DeviceIdType.MESH,
        ).start()

    def send_early(t0, count):
        for d in range(t0 // rows, (t0 + count) // rows):

            @pl.when(jnp.logical_and(late, me != d))
            def _():
                send(d)

    def send_on(d, carry):
        send(d)
        return carry

    work_small(0)

    @pl.when(late)
    def _():
        pl.semaphore_wait(barrier, n - 1)

    send_early(0, small)
    others.wait()
    for t0 in range(small, CHUNK, small):
        work_small(t0)
        send_early(t0, small)
    for t0 in range(CHUNK, templ, CHUNK):
        work(t0)
        send_early(t0, CHUNK)

    @pl.when(jnp.logical_not(late))
    def _():
        pl.semaphore_wait(barrier, n - 1)
        lax.fori_loop(0, me, send_on, 0)
        lax.fori_loop(me + 1, n, send_on, 0)

    rest = recv.at[pl.ds(1, n - 1)]
    pltpu.make_async_copy(rest, rest, recv_sem).wait()
    pltpu.make_async_copy(rest, rest, send_sem).wait()
    out_ref[...] = total[me] + jnp.sum(recv[pl.ds(1, n - 1)], axis=0)


def body(records, templates, shifts, present):
    n = lax.axis_size("sta")
    templ, local = templates.shape[0], templates.shape[1]
    rows = templ // n
    records = records.transpose(1, 0, 2)
    templates = templates.transpose(0, 2, 1, 3)
    energy_rows = -(-local * (WIDE // LANES) // 16) * 16
    hbm = pl.BlockSpec(memory_space=pl.ANY)
    return pl.pallas_call(
        functools.partial(kernel, n),
        out_shape=jax.ShapeDtypeStruct((rows, OUT), jnp.float32),
        in_specs=[hbm] * 4,
        out_specs=pl.BlockSpec(memory_space=pltpu.VMEM),
        scratch_shapes=[
            pltpu.VMEM(records.shape, records.dtype),
            pltpu.VMEM(templates.shape, templates.dtype),
            pltpu.VMEM((3 * TAPS, templ * local, LANES), jnp.float32),
            pltpu.VMEM(shifts.shape, shifts.dtype),
            pltpu.SMEM(present.shape, present.dtype),
            pltpu.VMEM((-(-3 * local // 8) * 8, WIDE), jnp.float32),
            pltpu.VMEM((local, 3, SUB, WIDE), jnp.bfloat16),
            pltpu.VMEM((energy_rows, LANES), jnp.float32),
            pltpu.VMEM((LANES, 4 * LANES), jnp.bfloat16),
            pltpu.VMEM((energy_rows, 4 * LANES), jnp.float32),
            pltpu.VMEM((energy_rows, LANES), jnp.float32),
            pltpu.VMEM((templ * local, LANES), jnp.int32),
            pltpu.VMEM((8, LANES), jnp.float32),
            pltpu.VMEM((len(LEVELS), 2 * CHUNK, LANES), jnp.bfloat16),
            pltpu.VMEM((n, rows, OUT), jnp.float32),
            pltpu.VMEM((n, rows, OUT), jnp.float32),
            pltpu.SemaphoreType.DMA((4,)),
            pltpu.SemaphoreType.DMA,
            pltpu.SemaphoreType.DMA,
        ],
        compiler_params=pltpu.CompilerParams(collective_id=0, vmem_limit_bytes=16 << 20, has_side_effects=True),
    )(*[
        pltpu.with_memory_space_constraint(x, pltpu.HBM) for x in (records, templates, shifts, present)])


def solution(mesh):
    placed = (P("sta", None, "parts"), P(None, "sta", None, None), P(), P())
    return jax.shard_map(
        body, mesh=mesh, in_specs=placed, out_specs=P("sta", "parts"), check_vma=False
    )
```
